512 devices in a mesh: gx: 32 (over x, y, core), gy: 16 (over z).
Axes of the slice: x: 4, y: 4, z: 16, core: 2. Of those that a mesh axis runs over, the one named last changes fastest.
Arguments:
- schur_blocks: float32 [32, 16, 768, 768], P('gx', 'gy'), may hold values from -32 to 32, as said below
- basis: float32 [32, 16, 32, 768], P('gx', 'gy'), may hold values from -0.21875 to 0.21875
- loads: float32 [32, 16, 16, 768], P('gx', 'gy'), may hold values from -64 to 64
- coarse_inverse: float32 [16384, 16384], P(('gx', 'gy')), may hold values from -0.09375 to 0.09375
- iface_map: int32 [32, 16, 768], P('gx', 'gy'), may hold values from 0 to 767, as said below
- coarse_slot: int32 [512], replicated, may hold values from 0 to 511, each once
Outputs:
- solution: float32 [32, 16, 16, 768], P('gx', 'gy')
The draws below stay inside these ranges and needn't reach their ends.
Inputs may be any that keep to these rules, and one draw needn't show every extreme that they name: `schur_blocks`: each block is symmetric. `iface_map`: for every subdomain the map is a permutation of 0 to 767 that maps each aligned block of 128 cells onto itself. `coarse_slot`: every subdomain has its own coarse block number.
All inputs are finite; a program needn't handle non-finite values.
Results may differ from the reference program's by a relative error of at most 0.0001.
Values sent between devices are 32-bit elements; how exact they have to be, the bound alone decides.
No kernel may reach another device: no remote copies, remote signals or barrier semaphores. Data moves between devices by JAX's collectives and lax.ppermute only.
A program may use at most 128 MiB of HBM per device.

```python
import math
import jax
import jax.numpy as jnp
from jax import lax

EW = 256
ES = 128
MB = 128
K = 32
LOADS = 16
ITERS = 3
SB = 768
NX = 32
NY = 16
SUBS = 512
NC = 16384


def draw_schur_blocks(key, part):
    low_end, high_end, diagonal_level, coupling = (0.5, 5.0, 2.0, 0.5)

    def one_block(block_index):
        sub_key = jax.random.fold_in(key, block_index)
        first_key, second_key = jax.random.split(sub_key)
        permeability = jnp.exp(jax.random.uniform(first_key, (SB,), jnp.float32, math.log(low_end), math.log(high_end)))
        noise = jax.random.normal(second_key, (SB, SB), jnp.float32)
        symmetric = (noise + noise.T) * (coupling / math.sqrt(2.0 * SB))
        centred = symmetric + diagonal_level * jnp.eye(SB, dtype=jnp.float32)
        root_scale = jnp.sqrt(permeability)
        return root_scale[:, None] * centred * root_scale[None, :]
    blocks = lax.map(one_block, jnp.arange(NX * NY, dtype=jnp.int32))
    return blocks.reshape(NX, NY, SB, SB).astype(jnp.float32)


def draw_loads(key, part):
    block_count = NX * NY
    first_key, second_key = jax.random.split(jax.random.fold_in(key, 7), 2)
    ramp = jnp.arange(block_count, dtype=jnp.float32) / max(block_count - 1, 1)
    rough = jnp.exp(jax.random.uniform(second_key, (NX, NY, 1, SB), jnp.float32, math.log(0.5), math.log(2.0)))
    rise = jnp.exp(math.log(3.0) * ramp).reshape(NX, NY, 1, 1)
    base = jnp.clip(jax.random.normal(first_key, (NX, NY, LOADS, SB), jnp.float32), -4.0, 4.0)
    return (base * rough * rise).astype(jnp.float32)


def draw_iface_map(key, part):
    scores = jax.random.randint(jax.random.fold_in(key, 11), (NX, NY, SB // MB, MB), 0, 65536, jnp.int32) * MB + jnp.arange(MB, dtype=jnp.int32)
    order = jnp.argsort(scores, axis=3).astype(jnp.int32)
    offsets = (jnp.arange(SB // MB, dtype=jnp.int32) * MB)[:, None]
    return (order + offsets).reshape(NX, NY, SB).astype(jnp.int32)


def shard_levels(rng, extent, cuts, least, largest):
    level = 1.0
    for dim, blocks in cuts:
        steps = jax.random.uniform(jax.random.fold_in(jax.random.fold_in(rng, 6), dim), (blocks,), jnp.float32, least / len(cuts), largest / len(cuts))
        level = level * jnp.repeat(jnp.exp(steps), extent[dim] // blocks).reshape((-1,) + (1,) * (len(extent) - 1 - dim))
    return level


def normal_values(stream_key, dims, scale, limit, pieces=(), kind=jnp.bfloat16):
    result = scale * jax.random.normal(stream_key, dims, jnp.float32)
    if pieces:
        result = result * shard_levels(stream_key, dims, pieces, -0.22, 0.18)
    return jnp.clip(result, -limit, limit).astype(kind)


def setup_inputs(seed: int = 0) -> dict:
    streams_of = jax.random.split(jax.random.key(seed), 7)
    return {
        "schur_blocks": draw_schur_blocks(jax.random.fold_in(streams_of[6], 71), 0),
        "basis": normal_values(streams_of[1], (NX, NY, K, SB), SB ** -0.5, 0.21875, ((0, 32), (1, 16)), jnp.float32),
        "loads": draw_loads(jax.random.fold_in(streams_of[6], 71), 0),
        "coarse_inverse": normal_values(streams_of[3], (NC, NC), (NC // 4) ** -0.5, 0.09375, ((0, 512),), jnp.float32),
        "iface_map": draw_iface_map(jax.random.fold_in(streams_of[6], 71), 0),
        "coarse_slot": jax.random.permutation(streams_of[5], SUBS).astype(jnp.int32),
    }


highest = lax.Precision.HIGHEST
epsilon = 1e-6


def permute(values, index):
    return jnp.take_along_axis(values, jnp.broadcast_to(index[:, :, None, :], values.shape), axis=3)


def assemble(values, iface_map, inverse):
    layout = permute(values, inverse)
    west_edge = layout[..., :EW]
    east_edge = layout[..., EW:2 * EW]
    south_edge = layout[..., 2 * EW:2 * EW + ES]
    north_edge = layout[..., 2 * EW + ES:]
    from_west = jnp.concatenate([jnp.zeros_like(east_edge[:, :1]), east_edge[:, :-1]], axis=1)
    from_east = jnp.concatenate([west_edge[:, 1:], jnp.zeros_like(west_edge[:, :1])], axis=1)
    from_south = jnp.concatenate([jnp.zeros_like(north_edge[:1]), north_edge[:-1]], axis=0)
    from_north = jnp.concatenate([south_edge[1:], jnp.zeros_like(south_edge[:1])], axis=0)
    outside = jnp.concatenate([from_west, from_east, from_south, from_north], axis=3)
    return values + permute(outside, iface_map)


def reference(schur_blocks, basis, loads, coarse_inverse, iface_map, coarse_slot):
    inverse = jnp.argsort(iface_map, axis=2).astype(jnp.int32)
    slot_inverse = jnp.argsort(coarse_slot).astype(jnp.int32)
    domain_count = NX * NY
    residual = assemble(loads, iface_map, inverse)
    solution = jnp.zeros_like(residual)
    for iteration in range(ITERS):
        coeffs = jnp.einsum('abkp,ablp->ablk', basis, residual, precision=highest)
        flat = jnp.transpose(coeffs.reshape(domain_count, LOADS, K), (1, 0, 2))
        ordered = flat[:, slot_inverse, :].reshape(LOADS, domain_count * K)
        lifted_all = lax.dot_general(ordered, coarse_inverse, (((1,), (1,)), ((), ())), precision=highest, preferred_element_type=jnp.float32)
        lifted = jnp.transpose(lifted_all.reshape(LOADS, domain_count, K), (1, 0, 2)).reshape(NX, NY, LOADS, K)
        spread = jnp.einsum('ablk,abkp->ablp', lifted, basis, precision=highest)
        search = residual + assemble(spread, iface_map, inverse)
        local_image = jnp.einsum('ablp,abpq->ablq', search, schur_blocks, precision=highest)
        applied = assemble(local_image, iface_map, inverse)
        numerator = jnp.sum(residual * applied, axis=(0, 1, 3))
        denominator = jnp.sum(applied * applied, axis=(0, 1, 3))
        stride = (numerator / (denominator + epsilon))[:, None]
        solution = solution + stride * search
        residual = residual - stride * applied
    return solution
```

```python
import functools
import jax
import jax.numpy as jnp
from jax import lax
from jax.experimental import pallas as pl
from jax.experimental.pallas import tpu as pltpu
from jax.sharding import PartitionSpec as P

EW = 256
ES = 128
MB = 128
ITERS = 3
LANES = 128
ROWS = 8

highest = lax.Precision.HIGHEST
epsilon = 1e-06
VMEM = pl.BlockSpec(memory_space=pltpu.VMEM)
SMEM = pl.BlockSpec(memory_space=pltpu.SMEM)


def dot(a, b, dims=((1,), (0,))):
    return lax.dot_general(
        a, b, (dims, ((), ())), precision=highest, preferred_element_type=jnp.float32
    )


def call(kernel, outs, args, flops=1 << 20, specs=None):
    outs = [jax.ShapeDtypeStruct(shape, dtype) for shape, dtype in outs]
    moved = sum(a.size * a.dtype.itemsize for a in args) + sum(
        o.size * o.dtype.itemsize for o in outs
    )
    return pl.pallas_call(
        kernel,
        out_shape=outs,
        in_specs=specs or [VMEM] * len(args),
        out_specs=[VMEM] * len(outs),
        cost_estimate=pl.CostEstimate(flops=flops, bytes_accessed=moved, transcendentals=0),
    )(*args)


def sides(cells):
    return ((0, EW), (EW, 2 * EW), (2 * EW, 2 * EW + ES), (2 * EW + ES, cells))


def sublane_mask(rows, loads):
    row = lax.broadcasted_iota(jnp.int32, (rows, LANES), 0)
    lane = lax.broadcasted_iota(jnp.int32, (rows, LANES), 1)
    return lax.rem(row, ROWS) == lax.div(lane, loads)


def pack(rows, loads):
    kept = jnp.where(sublane_mask(rows.shape[0], loads), rows, 0.0)
    return jnp.sum(kept.reshape(rows.shape[0] // ROWS, ROWS, LANES), axis=1)


def column_of(row, loads):
    a = lax.broadcasted_iota(jnp.int32, (loads, LANES), 0)
    b = lax.broadcasted_iota(jnp.int32, (loads, LANES), 1)
    return jnp.sum(jnp.where(a == b, row, 0.0), axis=1, keepdims=True)


def row_of(column, loads):
    a = lax.broadcasted_iota(jnp.int32, (loads, LANES), 0)
    b = lax.broadcasted_iota(jnp.int32, (loads, LANES), 1)
    return jnp.sum(jnp.where(a == lax.rem(b, loads), column, 0.0), axis=0, keepdims=True)


def one_hot(map_row, block):
    inside = map_row[:, block * MB : (block + 1) * MB] - block * MB
    spot = lax.broadcasted_iota(jnp.int32, (MB, MB), 0)
    return jnp.where(spot == inside, 1.0, 0.0)


def route_kernel(slot_ref, rows_ref, out_ref):
    groups, modes, width = out_ref.shape
    per_tile = LANES // modes
    tiles = width // LANES
    lane = lax.broadcasted_iota(jnp.int32, (modes, LANES), 1)

    def step(group, carry):
        for tile in range(tiles):
            block = jnp.zeros((modes, LANES), jnp.float32)
            for part in range(per_tile):
                slot = slot_ref[(group * tiles + tile) * per_tile + part]
                home = lax.div(slot, per_tile)
                offset = lax.rem(slot, per_tile)
                source = rows_ref[:, pl.ds(pl.multiple_of(home * LANES, LANES), LANES)]
                shift = lax.rem(part - offset + per_tile, per_tile) * modes
                moved = pltpu.roll(source, shift, 1)
                block = jnp.where(lax.div(lane, modes) == part, moved, block)
            out_ref[group, :, tile * LANES : (tile + 1) * LANES] = block
        return carry

    lax.fori_loop(0, groups, step, 0)


def prepare_kernel(map_ref, schur_ref, basis_ref, loads_ref, s_ref, b_ref, *edge_refs):
    cells = schur_ref.shape[0]
    map_row = map_ref[...]
    hots = [one_hot(map_row, block) for block in range(cells // MB)]
    for block, hot in enumerate(hots):
        span = slice(block * MB, (block + 1) * MB)
        b_ref[:, span] = dot(basis_ref[:, span], hot, ((1,), (1,)))
        moved = dot(loads_ref[:, span], hot, ((1,), (1,)))
        for edge_ref, (low, high) in zip(edge_refs, sides(cells)):
            if low <= block * MB < high:
                edge_ref[:, block * MB - low : (block + 1) * MB - low] = moved
    for i, left in enumerate(hots):
        rows = dot(left, schur_ref[i * MB : (i + 1) * MB, :])
        for j, right in enumerate(hots):
            span = slice(j * MB, (j + 1) * MB)
            s_ref[i * MB : (i + 1) * MB, span] = dot(rows[:, span], right, ((1,), (1,)))


def joined(own, other):
    return jnp.concatenate([a[...] + b[...] for a, b in zip(own, other)], axis=1)


def gather_kernel(has_dots, has_coeffs, *refs):
    refs = list(refs)
    own, other = refs[:4], refs[4:8]
    refs = refs[8:]
    residual_ref = refs.pop(0) if has_dots else None
    basis_ref = refs.pop(0) if has_coeffs else None
    field_ref, out_ref = refs
    field = joined(own, other)
    loads = field.shape[0]
    field_ref[...] = field
    parts = []
    if has_coeffs:
        copies = jnp.concatenate([field] * (LANES // loads), axis=0)
        parts.append(pack(dot(basis_ref[...], copies, ((1,), (1,))), loads))
    else:
        parts.append(jnp.zeros((4, LANES), jnp.float32))
    if has_dots:
        for other_field in (residual_ref[...], field):
            total = jnp.sum(other_field * field, axis=1, keepdims=True)
            parts.append(row_of(total, loads))
    else:
        parts.append(jnp.zeros((2, LANES), jnp.float32))
    parts.append(jnp.zeros((2, LANES), jnp.float32))
    payload = jnp.concatenate(parts, axis=0)
    out_ref[...] = jnp.broadcast_to(payload[None], out_ref.shape)


def coarse_kernel(loads, gathered_ref, matrix_ref, out_ref, wide_ref):
    columns = gathered_ref.shape[0]
    groups = out_ref.shape[0]
    modes = matrix_ref.shape[0] // groups
    quads = modes // ROWS
    keep = sublane_mask(ROWS, loads)
    for column in range(columns):
        for quad in range(quads):
            row = gathered_ref[column, quad : quad + 1, :]
            start = (column * quads + quad) * ROWS
            wide_ref[start : start + ROWS, :] = jnp.where(keep, row, 0.0)
    product = dot(matrix_ref[...], wide_ref[...])
    a = lax.broadcasted_iota(jnp.int32, (LANES, LANES), 0)
    b = lax.broadcasted_iota(jnp.int32, (LANES, LANES), 1)
    fold = jnp.where(lax.rem(a, loads) == lax.rem(b, loads), 1.0, 0.0)
    packed = pack(dot(product, fold), loads)
    tail = jnp.sum(gathered_ref[...], axis=0)[quads:, :]
    for group in range(groups):
        out_ref[group, :quads, :] = packed[group * quads : (group + 1) * quads, :]
        out_ref[group, quads:, :] = tail


def lift_kernel(first, *refs):
    refs = list(refs)
    reduced_ref, basis_ref, residual_ref = refs[:3]
    refs = refs[3:]
    if not first:
        image_ref, solution_ref, search_ref, lifted_ref = refs[:4]
        refs = refs[4:]
        residual_out, solution_out = refs[:2]
        refs = refs[2:]
    lifted_out, edges = refs[0], refs[1:]
    loads, cells = residual_ref.shape
    modes = basis_ref.shape[0]
    quads = modes // ROWS
    sums = jnp.sum(reduced_ref[...], axis=0)
    lifted = sums[:quads, :]
    if not first:
        stride_row = sums[quads : quads + 1, :] / (sums[quads + 1 : quads + 2, :] + epsilon)
        stride = column_of(stride_row, loads)
        residual_out[...] = residual_ref[...] - stride * image_ref[...]
        solution_out[...] = solution_ref[...] + stride * search_ref[...]
        lifted = lifted_ref[...] - stride_row * lifted
    lifted_out[...] = lifted
    keep = sublane_mask(ROWS, loads)
    wide = jnp.concatenate(
        [jnp.where(keep, lifted[quad : quad + 1, :], 0.0) for quad in range(quads)], axis=0
    )
    a = lax.broadcasted_iota(jnp.int32, (loads, LANES), 0)
    b = lax.broadcasted_iota(jnp.int32, (loads, LANES), 1)
    fold = jnp.where(a == lax.rem(b, loads), 1.0, 0.0)
    narrow = dot(fold, wide, ((1,), (1,)))
    spread = dot(narrow, basis_ref[...])
    for edge, (low, high) in zip(edges, sides(cells)):
        edge[...] = spread[:, low:high]


def schur_kernel(*refs):
    own, other = refs[:4], refs[4:8]
    residual_ref, schur_ref, search_ref = refs[8:11]
    edges = refs[11:]
    search = residual_ref[...] + joined(own, other)
    search_ref[...] = search
    image = dot(search, schur_ref[...])
    for edge, (low, high) in zip(edges, sides(search.shape[1])):
        edge[...] = image[:, low:high]


def total_kernel(gathered_ref, out_ref):
    out_ref[...] = jnp.broadcast_to(jnp.sum(gathered_ref[...], axis=0)[None], out_ref.shape)


def finish_kernel(reduced_ref, solution_ref, search_ref, map_ref, out_ref):
    loads, cells = solution_ref.shape
    sums = jnp.sum(reduced_ref[...], axis=0)
    stride = column_of(sums[4:5, :] / (sums[5:6, :] + epsilon), loads)
    result = solution_ref[...] + stride * search_ref[...]
    map_row = map_ref[...]
    for block in range(cells // MB):
        span = slice(block * MB, (block + 1) * MB)
        out_ref[:, span] = dot(result[:, span], one_hot(map_row, block))


def exchange(edges):
    west, east, south, north = edges
    found = []
    for axis, low, high in (("gy", west, east), ("gx", south, north)):
        count = lax.axis_size(axis)
        forward = [(i, i + 1) for i in range(count - 1)]
        backward = [(i + 1, i) for i in range(count - 1)]
        found.append(lax.ppermute(high, axis, forward))
        found.append(lax.ppermute(low, axis, backward))
    return found


def per_device(schur_blocks, basis, loads, coarse_inverse, iface_map, coarse_slot):
    f32 = jnp.float32
    columns = lax.axis_size("gy")
    groups = lax.axis_size("gx")
    count, cells = loads.shape[2:]
    modes = basis.shape[2]
    field = ((count, cells), f32)
    edge_shapes = [((count, high - low), f32) for low, high in sides(cells)]
    packed = ((modes // ROWS, LANES), f32)
    along = ((columns, ROWS, LANES), f32)
    across = ((groups, ROWS, LANES), f32)

    (routed,) = call(
        route_kernel,
        [((groups, modes, columns * modes), f32)],
        [coarse_slot, coarse_inverse],
        specs=[SMEM, VMEM],
    )
    matrix = lax.all_to_all(routed, "gx", 0, 0, tiled=True)
    matrix = matrix.reshape(groups * modes, columns * modes)

    schur, modes_here, *edges = call(
        prepare_kernel,
        [((cells, cells), f32), ((modes, cells), f32), *edge_shapes],
        [iface_map[0], schur_blocks[0, 0], basis[0, 0], loads[0, 0]],
        flops=1 << 28,
    )
    residual, payload = call(
        functools.partial(gather_kernel, False, True),
        [field, along],
        [*edges, *exchange(edges), modes_here],
    )
    solution = image = search = lifted = None
    for iteration in range(ITERS):
        gathered = lax.all_to_all(payload, "gy", 0, 0, tiled=True)
        (partial,) = pl.pallas_call(
            functools.partial(coarse_kernel, count),
            out_shape=[jax.ShapeDtypeStruct(*across)],
            in_specs=[VMEM] * 2,
            out_specs=[VMEM],
            scratch_shapes=[pltpu.VMEM((columns * modes, LANES), f32)],
            cost_estimate=pl.CostEstimate(
                flops=1 << 29, bytes_accessed=1 << 22, transcendentals=0
            ),
        )(gathered, matrix)
        reduced = lax.all_to_all(partial, "gx", 0, 0, tiled=True)
        if iteration == 0:
            lifted, *edges = call(
                functools.partial(lift_kernel, True),
                [packed, *edge_shapes],
                [reduced, modes_here, residual],
            )
            solution = jnp.zeros((count, cells), f32)
        else:
            residual, solution, lifted, *edges = call(
                functools.partial(lift_kernel, False),
                [field, field, packed, *edge_shapes],
                [reduced, modes_here, residual, image, solution, search, lifted],
            )
        search, *images = call(
            schur_kernel,
            [field, *edge_shapes],
            [*edges, *exchange(edges), residual, schur],
            flops=1 << 27,
        )
        more = iteration < ITERS - 1
        image, payload = call(
            functools.partial(gather_kernel, True, more),
            [field, along],
            [*images, *exchange(images), residual] + ([modes_here] if more else []),
        )
    gathered = lax.all_to_all(payload, "gy", 0, 0, tiled=True)
    (partial,) = call(total_kernel, [across], [gathered])
    reduced = lax.all_to_all(partial, "gx", 0, 0, tiled=True)
    (result,) = call(finish_kernel, [field], [reduced, solution, search, iface_map[0]])
    return result[None, None]


def solution(mesh):
    placed = (
        P("gx", "gy", None, None),
        P("gx", "gy", None, None),
        P("gx", "gy", None, None),
        P(("gx", "gy"), None),
        P("gx", "gy", None),
        P(),
    )
    return jax.shard_map(
        per_device, mesh=mesh, in_specs=placed, out_specs=P("gx", "gy", None, None), check_vma=False
    )
```

```python
import functools
import jax
import jax.numpy as jnp
from jax import lax
from jax.experimental import pallas as pl
from jax.experimental.pallas import tpu as pltpu
from jax.sharding import PartitionSpec as P

EW = 256
ES = 128
MB = 128
ITERS = 3
LANES = 128
ROWS = 8
LIMIT = 20 << 20

highest = lax.Precision.HIGHEST
epsilon = 1e-06
VMEM = pl.BlockSpec(memory_space=pltpu.VMEM)
SMEM = pl.BlockSpec(memory_space=pltpu.SMEM)


def dot(a, b, dims=((1,), (0,))):
    return lax.dot_general(
        a, b, (dims, ((), ())), precision=highest, preferred_element_type=jnp.float32
    )


def split(value):
    high = value.astype(jnp.bfloat16)
    return high, (value - high.astype(jnp.float32)).astype(jnp.bfloat16)


def narrow_dot(a, b, dims=((1,), (0,))):
    return lax.dot_general(a, b, (dims, ((), ())), preferred_element_type=jnp.float32)


def call(kernel, outs, args, flops=1 << 20, specs=None, scratch=()):
    outs = [jax.ShapeDtypeStruct(shape, dtype) for shape, dtype in outs]
    moved = sum(a.size * a.dtype.itemsize for a in args) + sum(
        o.size * o.dtype.itemsize for o in outs
    )
    return pl.pallas_call(
        kernel,
        out_shape=outs,
        in_specs=specs or [VMEM] * len(args),
        out_specs=[VMEM] * len(outs),
        scratch_shapes=scratch,
        compiler_params=pltpu.CompilerParams(vmem_limit_bytes=LIMIT),
        cost_estimate=pl.CostEstimate(flops=flops, bytes_accessed=moved, transcendentals=0),
    )(*args)


def sides(cells):
    return ((0, EW), (EW, 2 * EW), (2 * EW, 2 * EW + ES), (2 * EW + ES, cells))


def sublane_mask(rows, loads):
    row = lax.broadcasted_iota(jnp.int32, (rows, LANES), 0)
    lane = lax.broadcasted_iota(jnp.int32, (rows, LANES), 1)
    return lax.rem(row, ROWS) == lax.div(lane, loads)


def pack(rows, loads):
    kept = jnp.where(sublane_mask(rows.shape[0], loads), rows, 0.0)
    return jnp.sum(kept.reshape(rows.shape[0] // ROWS, ROWS, LANES), axis=1)


def column_of(row, loads):
    a = lax.broadcasted_iota(jnp.int32, (loads, LANES), 0)
    b = lax.broadcasted_iota(jnp.int32, (loads, LANES), 1)
    return jnp.sum(jnp.where(a == b, row, 0.0), axis=1, keepdims=True)


def row_of(column, loads):
    a = lax.broadcasted_iota(jnp.int32, (loads, LANES), 0)
    b = lax.broadcasted_iota(jnp.int32, (loads, LANES), 1)
    return jnp.sum(jnp.where(a == lax.rem(b, loads), column, 0.0), axis=0, keepdims=True)


def one_hot(map_row, block):
    inside = map_row[:, block * MB : (block + 1) * MB] - block * MB
    spot = lax.broadcasted_iota(jnp.int32, (MB, MB), 0)
    return jnp.where(spot == inside, 1.0, 0.0)


def route_kernel(slot_ref, rows_ref, out_ref, token_ref):
    groups, modes, width = out_ref.shape
    per_tile = LANES // modes
    tiles = width // LANES
    lane = lax.broadcasted_iota(jnp.int32, (modes, LANES), 1)

    def step(group, carry):
        for tile in range(tiles):
            block = jnp.zeros((modes, LANES), jnp.float32)
            for part in range(per_tile):
                slot = slot_ref[(group * tiles + tile) * per_tile + part]
                home = lax.div(slot, per_tile)
                offset = lax.rem(slot, per_tile)
                source = rows_ref[:, pl.ds(pl.multiple_of(home * LANES, LANES), LANES)]
                shift = lax.rem(part - offset + per_tile, per_tile) * modes
                moved = pltpu.roll(source, shift, 1)
                block = jnp.where(lax.div(lane, modes) == part, moved, block)
            out_ref[group, :, tile * LANES : (tile + 1) * LANES] = block
        return carry

    lax.fori_loop(0, groups, step, 0)
    token_ref[...] = jnp.zeros_like(token_ref)


def prepare_kernel(map_ref, basis_ref, loads_ref, token_ref, b_ref, *edge_refs):
    modes, cells = basis_ref.shape
    map_row = map_ref[...]
    for block in range(cells // MB):
        hot = one_hot(map_row, block)
        span = slice(block * MB, (block + 1) * MB)
        high, low = split(dot(basis_ref[:, span], hot, ((1,), (1,))))
        b_ref[:modes, span] = high
        b_ref[modes:, span] = low
        moved = dot(loads_ref[:, span], hot, ((1,), (1,)))
        for edge_ref, (start, stop) in zip(edge_refs, sides(cells)):
            if start <= block * MB < stop:
                edge_ref[:, block * MB - start : (block + 1) * MB - start] = moved


def reorder_kernel(map_ref, schur_ref, token_ref, high_ref, low_ref):
    cells = schur_ref.shape[0]
    map_row = map_ref[...]
    hots = [one_hot(map_row, block).astype(jnp.bfloat16) for block in range(cells // MB)]
    for i, left in enumerate(hots):
        span_i = slice(i * MB, (i + 1) * MB)
        for part, out_ref in zip(split(schur_ref[span_i, :]), (high_ref, low_ref)):
            rows = narrow_dot(left, part).astype(jnp.bfloat16)
            for j, right in enumerate(hots):
                span = slice(j * MB, (j + 1) * MB)
                out_ref[span_i, span] = narrow_dot(rows[:, span], right, ((1,), (1,))).astype(
                    jnp.bfloat16
                )


def joined(own, other):
    return jnp.concatenate([a[...] + b[...] for a, b in zip(own, other)], axis=1)


def gather_kernel(has_dots, has_coeffs, *refs):
    refs = list(refs)
    own, other = refs[:4], refs[4:8]
    refs = refs[8:]
    residual_ref = refs.pop(0) if has_dots else None
    basis_ref = refs.pop(0) if has_coeffs else None
    field_ref, out_ref = refs
    field = joined(own, other)
    loads = field.shape[0]
    field_ref[...] = field
    parts = []
    if has_coeffs:
        modes = basis_ref.shape[0] // 2
        copies = [jnp.concatenate([part] * (LANES // loads), axis=0) for part in split(field)]
        both = narrow_dot(basis_ref[...], jnp.concatenate(copies, axis=0), ((1,), (1,)))
        both = both[:, :LANES] + both[:, LANES:]
        parts.append(pack(both[:modes] + both[modes:], loads))
    else:
        parts.append(jnp.zeros((4, LANES), jnp.float32))
    if has_dots:
        for other_field in (residual_ref[...], field):
            total = jnp.sum(other_field * field, axis=1, keepdims=True)
            parts.append(row_of(total, loads))
    else:
        parts.append(jnp.zeros((2, LANES), jnp.float32))
    parts.append(jnp.zeros((2, LANES), jnp.float32))
    payload = jnp.concatenate(parts, axis=0)
    out_ref[...] = jnp.broadcast_to(payload[None], out_ref.shape)


def coarse_kernel(loads, first, *refs):
    if first:
        gathered_ref, matrix_ref, out_ref, high_ref, low_ref, wide_ref = refs
        high, low = split(matrix_ref[...])
        high_ref[...] = high
        low_ref[...] = low
    else:
        gathered_ref, high_ref, low_ref, out_ref, wide_ref = refs
        high, low = high_ref[...], low_ref[...]
    columns = gathered_ref.shape[0]
    groups = out_ref.shape[0]
    modes = high_ref.shape[0] // groups
    quads = modes // ROWS
    keep = sublane_mask(ROWS, loads)
    for column in range(columns):
        for quad in range(quads):
            row = gathered_ref[column, quad : quad + 1, :]
            start = (column * quads + quad) * ROWS
            wide_ref[start : start + ROWS, :] = jnp.where(keep, row, 0.0)
    wide = wide_ref[...]
    shift = LANES // 2
    while shift >= loads:
        wide = wide + pltpu.roll(wide, shift, 1)
        shift //= 2
    right = jnp.concatenate(split(wide), axis=1)
    product = narrow_dot(high, right) + narrow_dot(low, right)
    packed = pack(product[:, :LANES] + product[:, LANES:], loads)
    tail = jnp.sum(gathered_ref[...], axis=0)[quads:, :]
    for group in range(groups):
        out_ref[group, :quads, :] = packed[group * quads : (group + 1) * quads, :]
        out_ref[group, quads:, :] = tail


def lift_kernel(iteration, *refs):
    refs = list(refs)
    reduced_ref, basis_ref = refs[:2]
    refs = refs[2:]
    if iteration:
        residual_ref, image_ref, search_ref, lifted_ref = refs[:4]
        refs = refs[4:]
        solution_ref = refs.pop(0) if iteration > 1 else None
        residual_out, solution_out = refs[:2]
        refs = refs[2:]
    lifted_out, edges = refs[0], refs[1:]
    loads = edges[0].shape[0]
    modes, cells = basis_ref.shape[0] // 2, basis_ref.shape[1]
    quads = modes // ROWS
    sums = jnp.sum(reduced_ref[...], axis=0)
    lifted = sums[:quads, :]
    if iteration:
        stride_row = sums[quads : quads + 1, :] / (sums[quads + 1 : quads + 2, :] + epsilon)
        stride = column_of(stride_row, loads)
        residual_out[...] = residual_ref[...] - stride * image_ref[...]
        step = stride * search_ref[...]
        solution_out[...] = step if solution_ref is None else solution_ref[...] + step
        lifted = lifted_ref[...] - stride_row * lifted
    lifted_out[...] = lifted
    keep = sublane_mask(ROWS, loads)
    wide = jnp.concatenate(
        [jnp.where(keep, lifted[quad : quad + 1, :], 0.0) for quad in range(quads)], axis=0
    )
    a = lax.broadcasted_iota(jnp.int32, (loads, LANES), 0)
    b = lax.broadcasted_iota(jnp.int32, (loads, LANES), 1)
    fold = jnp.where(a == lax.rem(b, loads), 1.0, 0.0)
    high, low = split(dot(fold, wide, ((1,), (1,))))
    left = jnp.concatenate(
        [jnp.concatenate([high, high], axis=1), jnp.concatenate([low, low], axis=1)], axis=0
    )
    both = narrow_dot(left, basis_ref[...])
    spread = both[:loads] + both[loads:]
    for edge, (start, stop) in zip(edges, sides(cells)):
        edge[...] = spread[:, start:stop]


def schur_kernel(*refs):
    own, other = refs[:4], refs[4:8]
    residual_ref, high_ref, low_ref, search_ref = refs[8:12]
    edges = refs[12:]
    search = residual_ref[...] + joined(own, other)
    search_ref[...] = search
    loads, cells = search.shape
    left = jnp.concatenate(split(search), axis=0)
    for edge, (start, stop) in zip(edges, sides(cells)):
        both = narrow_dot(left, high_ref[:, start:stop]) + narrow_dot(left, low_ref[:, start:stop])
        edge[...] = both[:loads] + both[loads:]


def total_kernel(gathered_ref, out_ref):
    out_ref[...] = jnp.broadcast_to(jnp.sum(gathered_ref[...], axis=0)[None], out_ref.shape)


def finish_kernel(reduced_ref, solution_ref, search_ref, map_ref, out_ref):
    loads, cells = solution_ref.shape
    sums = jnp.sum(reduced_ref[...], axis=0)
    stride = column_of(sums[4:5, :] / (sums[5:6, :] + epsilon), loads)
    result = solution_ref[...] + stride * search_ref[...]
    map_row = map_ref[...]
    for block in range(cells // MB):
        span = slice(block * MB, (block + 1) * MB)
        out_ref[:, span] = dot(result[:, span], one_hot(map_row, block))


def exchange(edges):
    west, east, south, north = edges
    found = []
    for axis, low, high in (("gy", west, east), ("gx", south, north)):
        count = lax.axis_size(axis)
        forward = [(i, i + 1) for i in range(count - 1)]
        backward = [(i + 1, i) for i in range(count - 1)]
        found.append(lax.ppermute(high, axis, forward))
        found.append(lax.ppermute(low, axis, backward))
    return found


def per_device(schur_blocks, basis, loads, coarse_inverse, iface_map, coarse_slot):
    f32 = jnp.float32
    columns = lax.axis_size("gy")
    groups = lax.axis_size("gx")
    count, cells = loads.shape[2:]
    modes = basis.shape[2]
    field = ((count, cells), f32)
    edge_shapes = [((count, high - low), f32) for low, high in sides(cells)]
    packed = ((modes // ROWS, LANES), f32)
    along = ((columns, ROWS, LANES), f32)
    across = ((groups, ROWS, LANES), f32)

    routed, token = call(
        route_kernel,
        [((groups, modes, columns * modes), f32), ((ROWS, LANES), f32)],
        [coarse_slot, coarse_inverse],
        specs=[SMEM, VMEM],
    )
    matrix = lax.all_to_all(routed, "gx", 0, 0, tiled=True)
    matrix = matrix.reshape(groups * modes, columns * modes)

    frame, *edges = call(
        prepare_kernel,
        [((2 * modes, cells), jnp.bfloat16), *edge_shapes],
        [iface_map[0], basis[0, 0], loads[0, 0], token],
    )
    residual, payload = call(
        functools.partial(gather_kernel, False, True),
        [field, along],
        [*edges, *exchange(edges), frame],
    )
    schur = call(
        reorder_kernel,
        [((cells, cells), jnp.bfloat16)] * 2,
        [iface_map[0], schur_blocks[0, 0], token],
        flops=1 << 28,
    )
    split_shape = (matrix.shape, jnp.bfloat16)
    wide = [pltpu.VMEM((columns * modes, LANES), f32)]
    solution = image = search = lifted = None
    for iteration in range(ITERS):
        first = iteration == 0
        if first:
            payload, matrix, *schur = lax.optimization_barrier((payload, matrix, *schur))
        gathered = lax.all_to_all(payload, "gy", 0, 0, tiled=True)
        partial, *parts = call(
            functools.partial(coarse_kernel, count, first),
            [across] + [split_shape] * (2 * first),
            [gathered, matrix] if first else [gathered, *halves],
            flops=1 << 29,
            scratch=wide,
        )
        halves = parts if first else halves
        reduced = lax.all_to_all(partial, "gx", 0, 0, tiled=True)
        known = [residual, image, search, lifted] if iteration else []
        found = call(
            functools.partial(lift_kernel, iteration),
            [field] * (2 if iteration else 0) + [packed, *edge_shapes],
            [reduced, frame, *known] + ([solution] if iteration > 1 else []),
        )
        if iteration:
            residual, solution, *found = found
        lifted, *edges = found
        search, *images = call(
            schur_kernel,
            [field, *edge_shapes],
            [*edges, *exchange(edges), residual, *schur],
            flops=1 << 27,
        )
        more = iteration < ITERS - 1
        image, payload = call(
            functools.partial(gather_kernel, True, more),
            [field, along],
            [*images, *exchange(images), residual] + ([frame] if more else []),
        )
    gathered = lax.all_to_all(payload, "gy", 0, 0, tiled=True)
    (partial,) = call(total_kernel, [across], [gathered])
    reduced = lax.all_to_all(partial, "gx", 0, 0, tiled=True)
    (result,) = call(finish_kernel, [field], [reduced, solution, search, iface_map[0]])
    return result[None, None]


def solution(mesh):
    placed = (
        P("gx", "gy", None, None),
        P("gx", "gy", None, None),
        P("gx", "gy", None, None),
        P(("gx", "gy"), None),
        P("gx", "gy", None),
        P(),
    )
    return jax.shard_map(
        per_device, mesh=mesh, in_specs=placed, out_specs=P("gx", "gy", None, None), check_vma=False
    )
```

```python
import functools
import jax
import jax.numpy as jnp
from jax import lax
from jax.experimental import pallas as pl
from jax.experimental.pallas import tpu as pltpu
from jax.sharding import PartitionSpec as P

EW = 256
ES = 128
MB = 128
ITERS = 3
LANES = 128
ROWS = 8
LIMIT = 20 << 20

highest = lax.Precision.HIGHEST
epsilon = 1e-06
VMEM = pl.BlockSpec(memory_space=pltpu.VMEM)
SMEM = pl.BlockSpec(memory_space=pltpu.SMEM)


def dot(a, b, dims=((1,), (0,))):
    return lax.dot_general(
        a, b, (dims, ((), ())), precision=highest, preferred_element_type=jnp.float32
    )


def split(value):
    high = value.astype(jnp.bfloat16)
    return high, (value - high.astype(jnp.float32)).astype(jnp.bfloat16)


def narrow_dot(a, b, dims=((1,), (0,))):
    return lax.dot_general(a, b, (dims, ((), ())), preferred_element_type=jnp.float32)


def call(kernel, outs, args, flops=1 << 20, specs=None, scratch=()):
    outs = [jax.ShapeDtypeStruct(shape, dtype) for shape, dtype in outs]
    moved = sum(a.size * a.dtype.itemsize for a in args) + sum(
        o.size * o.dtype.itemsize for o in outs
    )
    return pl.pallas_call(
        kernel,
        out_shape=outs,
        in_specs=specs or [VMEM] * len(args),
        out_specs=[VMEM] * len(outs),
        scratch_shapes=scratch,
        compiler_params=pltpu.CompilerParams(vmem_limit_bytes=LIMIT),
        cost_estimate=pl.CostEstimate(flops=flops, bytes_accessed=moved, transcendentals=0),
    )(*args)


def sides(cells):
    return ((0, EW), (EW, 2 * EW), (2 * EW, 2 * EW + ES), (2 * EW + ES, cells))


def sublane_mask(rows, loads):
    row = lax.broadcasted_iota(jnp.int32, (rows, LANES), 0)
    lane = lax.broadcasted_iota(jnp.int32, (rows, LANES), 1)
    return lax.rem(row, ROWS) == lax.div(lane, loads)


def pack(rows, loads):
    kept = jnp.where(sublane_mask(rows.shape[0], loads), rows, 0.0)
    return jnp.sum(kept.reshape(rows.shape[0] // ROWS, ROWS, LANES), axis=1)


def column_of(row, loads):
    a = lax.broadcasted_iota(jnp.int32, (loads, LANES), 0)
    b = lax.broadcasted_iota(jnp.int32, (loads, LANES), 1)
    return jnp.sum(jnp.where(a == b, row, 0.0), axis=1, keepdims=True)


def row_of(column, loads):
    a = lax.broadcasted_iota(jnp.int32, (loads, LANES), 0)
    b = lax.broadcasted_iota(jnp.int32, (loads, LANES), 1)
    return jnp.sum(jnp.where(a == lax.rem(b, loads), column, 0.0), axis=0, keepdims=True)


def one_hot(map_row, block):
    inside = map_row[:, block * MB : (block + 1) * MB] - block * MB
    spot = lax.broadcasted_iota(jnp.int32, (MB, MB), 0)
    return jnp.where(spot == inside, 1.0, 0.0)


def route_kernel(slot_ref, rows_ref, out_ref, token_ref):
    groups, modes, width = out_ref.shape
    per_tile = LANES // modes
    tiles = width // LANES
    owner = lax.broadcasted_iota(jnp.int32, (modes, LANES), 1) // modes

    def step(group, carry):
        for tile in range(tiles):
            block = jnp.zeros((modes, LANES), jnp.float32)
            for part in range(per_tile):
                slot = slot_ref[(group * tiles + tile) * per_tile + part]
                home = lax.shift_right_logical(slot, per_tile.bit_length() - 1)
                source = rows_ref[:, pl.ds(pl.multiple_of(home * LANES, LANES), LANES)]
                shift = ((part - slot) & (per_tile - 1)) * modes
                block = jnp.where(owner == part, pltpu.roll(source, shift, 1), block)
            out_ref[group, :, tile * LANES : (tile + 1) * LANES] = block
        return carry

    lax.fori_loop(0, groups, step, 0, unroll=2)
    token_ref[...] = jnp.zeros_like(token_ref)


def parities():
    return [lax.axis_index(axis) % 2 == 1 for axis in ("gy", "gx")]


def outgoing(field, refs):
    odd_column, odd_row = parities()
    west, east, south, north = (field[:, a:b] for a, b in sides(field.shape[1]))
    refs[0][...] = jnp.where(odd_column, west, east)
    refs[1][...] = jnp.where(odd_column, east, west)
    if len(refs) > 2:
        refs[2][...] = jnp.where(odd_row, south, north)
        refs[3][...] = jnp.where(odd_row, north, south)


def incoming(first, second, odd):
    return jnp.where(odd, first, second), jnp.where(odd, second, first)


def joined(field, others):
    odd_column, odd_row = parities()
    found = [*incoming(others[0], others[1], odd_column)]
    if len(others) > 2:
        found += incoming(others[2], others[3], odd_row)
    parts = [
        field[:, start:stop] + other for (start, stop), other in zip(sides(field.shape[1]), found)
    ]
    return jnp.concatenate(parts + [field[:, 2 * EW :]] * (len(others) == 2), axis=1)


def prepare_kernel(map_ref, basis_ref, loads_ref, token_ref, frame_ref, field_ref, *edge_refs):
    modes, cells = basis_ref.shape
    loads = loads_ref.shape[0]
    map_row = map_ref[...]
    both = jnp.concatenate([loads_ref[...], basis_ref[...]], axis=0)
    moved = jnp.concatenate(
        [
            dot(both[:, block * MB : (block + 1) * MB], one_hot(map_row, block), ((1,), (1,)))
            for block in range(cells // MB)
        ],
        axis=1,
    )
    high, low = split(moved[loads:])
    frame_ref[:modes, :] = high
    frame_ref[modes:, :] = low
    field_ref[...] = moved[:loads]
    outgoing(moved[:loads], edge_refs[:2])
    odd_row = parities()[1]
    south, north = (moved[:, start:stop] for start, stop in sides(cells)[2:])
    edge_refs[2][...] = jnp.where(odd_row, south, north)
    edge_refs[3][...] = jnp.where(odd_row, north, south)


def reorder_kernel(map_ref, schur_ref, token_ref, high_ref, low_ref):
    cells = schur_ref.shape[0]
    map_row = map_ref[...]
    hots = [one_hot(map_row, block).astype(jnp.bfloat16) for block in range(cells // MB)]
    for i, left in enumerate(hots):
        span_i = slice(i * MB, (i + 1) * MB)
        for part, out_ref in zip(split(schur_ref[span_i, :]), (high_ref, low_ref)):
            rows = narrow_dot(left, part).astype(jnp.bfloat16)
            for j, right in enumerate(hots):
                span = slice(j * MB, (j + 1) * MB)
                out_ref[span_i, span] = narrow_dot(rows[:, span], right, ((1,), (1,))).astype(
                    jnp.bfloat16
                )


def stacked(value):
    return jnp.concatenate(split(value), axis=0)


def coefficients(field, frame):
    loads, modes = field.shape[0], frame.shape[0] // 2
    copies = [jnp.concatenate([part] * (LANES // loads), axis=0) for part in split(field)]
    both = narrow_dot(frame, jnp.concatenate(copies, axis=0), ((1,), (1,)))
    both = both[:, :LANES] + both[:, LANES:]
    return pack(both[:modes] + both[modes:], loads)


def begin_kernel(own_ref, *refs):
    others = [ref[...] for ref in refs[:4]]
    frame_ref, residual_ref, out_ref, south_ref, north_ref = refs[4:]
    loads = own_ref.shape[0]
    south, north = incoming(others[2], others[3], parities()[1])
    south_ref[...] = stacked(south[loads:])
    north_ref[...] = stacked(north[loads:])
    field = joined(own_ref[...], others[:2] + [other[:loads] for other in others[2:]])
    residual_ref[...] = field
    coeffs = coefficients(field, frame_ref[...])
    payload = jnp.concatenate([coeffs, jnp.zeros_like(coeffs)], axis=0)
    out_ref[...] = jnp.broadcast_to(payload[None], out_ref.shape)


def gather_kernel(more, own_ref, *refs):
    others = [ref[...] for ref in refs[:4]]
    residual_ref, refs = refs[4], refs[5:]
    out_ref = refs[-1]
    field = joined(own_ref[...], others)
    loads = field.shape[0]
    if more:
        frame_ref, field_ref = refs[:2]
        field_ref[...] = field
        coeffs = coefficients(field, frame_ref[...])
    else:
        coeffs = jnp.zeros((4, LANES), jnp.float32)
    totals = [
        row_of(jnp.sum(other * field, axis=1, keepdims=True), loads)
        for other in (residual_ref[...], field)
    ]
    payload = jnp.concatenate([coeffs, *totals, jnp.zeros((2, LANES), jnp.float32)], axis=0)
    out_ref[...] = jnp.broadcast_to(payload[None], out_ref.shape)


def expanded(loads, gathered_ref, wide_ref):
    quads = wide_ref.shape[0] // (gathered_ref.shape[0] * ROWS)
    keep = sublane_mask(ROWS, loads)
    for column in range(gathered_ref.shape[0]):
        for quad in range(quads):
            row = gathered_ref[column, quad : quad + 1, :]
            start = (column * quads + quad) * ROWS
            wide_ref[start : start + ROWS, :] = jnp.where(keep, row, 0.0)
    wide = wide_ref[...]
    shift = LANES // 2
    while shift >= loads:
        wide = wide + pltpu.roll(wide, shift, 1)
        shift //= 2
    tail = jnp.sum(gathered_ref[...], axis=0)[quads:, :]
    return jnp.concatenate(split(wide), axis=1), tail


def coarse_kernel(loads, first, *refs):
    if first:
        gathered_ref, matrix_ref, out_ref, high_ref, low_ref, wide_ref = refs
        high, low = split(matrix_ref[...])
        high_ref[...] = high
        low_ref[...] = low
    else:
        gathered_ref, high_ref, low_ref, out_ref, wide_ref = refs
        high, low = high_ref[...], low_ref[...]
    right, tail = expanded(loads, gathered_ref, wide_ref)
    groups = out_ref.shape[0]
    quads = high_ref.shape[0] // (groups * ROWS)
    product = narrow_dot(high, right) + narrow_dot(low, right)
    packed = pack(product[:, :LANES] + product[:, LANES:], loads)
    nothing = jnp.zeros((quads, LANES), jnp.float32)
    blocks = [packed[group * quads : (group + 1) * quads, :] for group in range(groups)]
    blocks = [nothing, *blocks, nothing]
    for group in range(groups):
        out_ref[group] = jnp.concatenate(
            [blocks[group + 1], blocks[group], blocks[group + 2], tail], axis=0
        )


def lift_kernel(iteration, *refs):
    refs = list(refs)
    reduced_ref, frame_ref, south_ref, north_ref, residual_ref = refs[:5]
    refs = refs[5:]
    residual = residual_ref[...]
    loads, cells = residual.shape
    quads = frame_ref.shape[0] // (2 * ROWS)
    sums = jnp.sum(reduced_ref[...], axis=0)
    lifted = sums
    if iteration:
        image_ref, search_ref, lifted_ref = refs[:3]
        refs = refs[3:]
        solution_ref = refs.pop(0) if iteration > 1 else None
        residual_out, solution_out = refs[:2]
        refs = refs[2:]
        stride_row = sums[3 * quads : 3 * quads + 1, :] / (
            sums[3 * quads + 1 : 3 * quads + 2, :] + epsilon
        )
        stride = column_of(stride_row, loads)
        residual = residual - stride * image_ref[...]
        residual_out[...] = residual
        step = stride * search_ref[...]
        solution_out[...] = step if solution_ref is None else solution_ref[...] + step
        lifted = lifted_ref[...] - stride_row * sums
    lifted_out, base_out, edges = refs[0], refs[1], refs[2:]
    lifted_out[...] = lifted
    keep = sublane_mask(ROWS, loads)
    a = lax.broadcasted_iota(jnp.int32, (loads, LANES), 0)
    b = lax.broadcasted_iota(jnp.int32, (loads, LANES), 1)
    fold = jnp.where(a == lax.rem(b, loads), 1.0, 0.0).astype(jnp.bfloat16)

    def spread(part, other_frame):
        rows = lifted[part * quads : (part + 1) * quads, :]
        wide = jnp.concatenate(
            [jnp.where(keep, rows[quad : quad + 1, :], 0.0) for quad in range(quads)], axis=0
        )
        left = jnp.concatenate(
            [
                jnp.concatenate([half, half], axis=1)
                for half in (
                    narrow_dot(fold, piece, ((1,), (1,))).astype(jnp.bfloat16)
                    for piece in split(wide)
                )
            ],
            axis=0,
        )
        both = narrow_dot(left, other_frame)
        return both[:loads] + both[loads:]

    own = spread(0, frame_ref[...])
    outgoing(own, edges)
    base = residual + own
    low, middle = sides(cells)[2]
    base_out[:, :low] = base[:, :low]
    base_out[:, low:middle] = base[:, low:middle] + spread(1, south_ref[...])
    base_out[:, middle:] = base[:, middle:] + spread(2, north_ref[...])


def schur_kernel(base_ref, first_ref, second_ref, high_ref, low_ref, search_ref, image_ref, *edges):
    search = joined(base_ref[...], [first_ref[...], second_ref[...]])
    search_ref[...] = search
    loads = search.shape[0]
    left = stacked(search)
    both = narrow_dot(left, high_ref[...]) + narrow_dot(left, low_ref[...])
    image = both[:loads] + both[loads:]
    image_ref[...] = image
    outgoing(image, edges)


def total_kernel(gathered_ref, out_ref):
    out_ref[...] = jnp.broadcast_to(jnp.sum(gathered_ref[...], axis=0)[None], out_ref.shape)


def finish_kernel(reduced_ref, solution_ref, search_ref, map_ref, out_ref):
    loads, cells = solution_ref.shape
    sums = jnp.sum(reduced_ref[...], axis=0)
    stride = column_of(sums[4:5, :] / (sums[5:6, :] + epsilon), loads)
    result = solution_ref[...] + stride * search_ref[...]
    map_row = map_ref[...]
    for block in range(cells // MB):
        span = slice(block * MB, (block + 1) * MB)
        out_ref[:, span] = dot(result[:, span], one_hot(map_row, block))


def exchange(edges):
    found = []
    for number, edge in enumerate(edges):
        axis, start = ("gy", "gx")[number // 2], number % 2
        pairs = []
        for low in range(start, lax.axis_size(axis) - 1, 2):
            pairs += [(low, low + 1), (low + 1, low)]
        found.append(lax.ppermute(edge, axis, pairs))
    return found


def per_device(schur_blocks, basis, loads, coarse_inverse, iface_map, coarse_slot):
    f32, bf16 = jnp.float32, jnp.bfloat16
    columns = lax.axis_size("gy")
    groups = lax.axis_size("gx")
    count, cells = loads.shape[2:]
    modes = basis.shape[2]
    field = ((count, cells), f32)
    column_edges = [((count, EW), f32)] * 2
    edges_of = column_edges + [((count, ES), f32)] * 2
    packed = ((2 * ROWS, LANES), f32)
    along = ((columns, ROWS, LANES), f32)
    across = ((groups, 2 * ROWS, LANES), f32)

    routed, token = call(
        route_kernel,
        [((groups, modes, columns * modes), f32), ((ROWS, LANES), f32)],
        [coarse_slot, coarse_inverse],
        specs=[SMEM, VMEM],
    )
    matrix = lax.all_to_all(routed, "gx", 0, 0, tiled=True)
    matrix = matrix.reshape(groups * modes, columns * modes)

    frame, own, *edges = call(
        prepare_kernel,
        [((2 * modes, cells), bf16), field]
        + column_edges
        + [((count + modes, ES), f32)] * 2,
        [iface_map[0], basis[0, 0], loads[0, 0], token],
    )
    residual, payload, south, north = call(
        begin_kernel,
        [field, along] + [((2 * modes, ES), bf16)] * 2,
        [own, *exchange(edges), frame],
    )
    schur = call(
        reorder_kernel,
        [((cells, cells), bf16)] * 2,
        [iface_map[0], schur_blocks[0, 0], token],
        flops=1 << 28,
    )
    frames = [frame, south, north]
    split_shape = (matrix.shape, bf16)
    wide = [pltpu.VMEM((columns * modes, LANES), f32)]
    solution = image = search = lifted = None
    for iteration in range(ITERS):
        first = iteration == 0
        if first:
            payload, matrix, *schur = lax.optimization_barrier((payload, matrix, *schur))
        gathered = lax.all_to_all(payload, "gy", 0, 0, tiled=True)
        partial, *parts = call(
            functools.partial(coarse_kernel, count, first),
            [across] + [split_shape] * (2 * first),
            [gathered, matrix] if first else [gathered, *halves],
            flops=1 << 29,
            scratch=wide,
        )
        halves = parts if first else halves
        reduced = lax.all_to_all(partial, "gx", 0, 0, tiled=True)
        known = [image, search, lifted] if iteration else []
        found = call(
            functools.partial(lift_kernel, iteration),
            [field] * (2 if iteration else 0) + [packed, field, *column_edges],
            [reduced, *frames, residual, *known] + ([solution] if iteration > 1 else []),
        )
        if iteration:
            residual, solution, *found = found
        lifted, base, *edges = found
        search, local, *edges = call(
            schur_kernel,
            [field, field, *edges_of],
            [base, *exchange(edges), *schur],
            flops=1 << 27,
        )
        more = iteration < ITERS - 1
        found = call(
            functools.partial(gather_kernel, more),
            [field] * more + [along],
            [local, *exchange(edges), residual] + [frame] * more,
        )
        image, payload = found if more else (None, found[0])
    gathered = lax.all_to_all(payload, "gy", 0, 0, tiled=True)
    (partial,) = call(total_kernel, [((groups, ROWS, LANES), f32)], [gathered])
    reduced = lax.all_to_all(partial, "gx", 0, 0, tiled=True)
    (result,) = call(finish_kernel, [field], [reduced, solution, search, iface_map[0]])
    return result[None, None]


def solution(mesh):
    placed = (
        P("gx", "gy", None, None),
        P("gx", "gy", None, None),
        P("gx", "gy", None, None),
        P(("gx", "gy"), None),
        P("gx", "gy", None),
        P(),
    )
    return jax.shard_map(
        per_device, mesh=mesh, in_specs=placed, out_specs=P("gx", "gy", None, None), check_vma=False
    )
```

```python
import functools
import jax
import jax.numpy as jnp
from jax import lax
from jax.experimental import pallas as pl
from jax.experimental.pallas import tpu as pltpu
from jax.sharding import PartitionSpec as P

EW = 256
ES = 128
MB = 128
ITERS = 3
LANES = 128
ROWS = 8
LIMIT = 20 << 20

highest = lax.Precision.HIGHEST
epsilon = 1e-06
VMEM = pl.BlockSpec(memory_space=pltpu.VMEM)
SMEM = pl.BlockSpec(memory_space=pltpu.SMEM)


def dot(a, b, dims=((1,), (0,))):
    return lax.dot_general(
        a, b, (dims, ((), ())), precision=highest, preferred_element_type=jnp.float32
    )


def split(value):
    high = value.astype(jnp.bfloat16)
    return high, (value - high.astype(jnp.float32)).astype(jnp.bfloat16)


def narrow_dot(a, b, dims=((1,), (0,))):
    return lax.dot_general(a, b, (dims, ((), ())), preferred_element_type=jnp.float32)


def call(kernel, outs, args, flops=1 << 20, specs=None, scratch=()):
    outs = [jax.ShapeDtypeStruct(shape, dtype) for shape, dtype in outs]
    moved = sum(a.size * a.dtype.itemsize for a in args) + sum(
        o.size * o.dtype.itemsize for o in outs
    )
    return pl.pallas_call(
        kernel,
        out_shape=outs,
        in_specs=specs or [VMEM] * len(args),
        out_specs=[VMEM] * len(outs),
        scratch_shapes=scratch,
        compiler_params=pltpu.CompilerParams(vmem_limit_bytes=LIMIT),
        cost_estimate=pl.CostEstimate(flops=flops, bytes_accessed=moved, transcendentals=0),
    )(*args)


def sides(cells):
    return ((0, EW), (EW, 2 * EW), (2 * EW, 2 * EW + ES), (2 * EW + ES, cells))


def sublane_mask(rows, loads):
    row = lax.broadcasted_iota(jnp.int32, (rows, LANES), 0)
    lane = lax.broadcasted_iota(jnp.int32, (rows, LANES), 1)
    return lax.rem(row, ROWS) == lax.div(lane, loads)


def pack(rows, loads):
    kept = jnp.where(sublane_mask(rows.shape[0], loads), rows, 0.0)
    return jnp.sum(kept.reshape(rows.shape[0] // ROWS, ROWS, LANES), axis=1)


def column_of(row, loads):
    a = lax.broadcasted_iota(jnp.int32, (loads, LANES), 0)
    b = lax.broadcasted_iota(jnp.int32, (loads, LANES), 1)
    return jnp.sum(jnp.where(a == b, row, 0.0), axis=1, keepdims=True)


def row_of(column, loads):
    a = lax.broadcasted_iota(jnp.int32, (loads, LANES), 0)
    b = lax.broadcasted_iota(jnp.int32, (loads, LANES), 1)
    return jnp.sum(jnp.where(a == lax.rem(b, loads), column, 0.0), axis=0, keepdims=True)


def one_hot(map_row, block):
    inside = map_row[:, block * MB : (block + 1) * MB] - block * MB
    spot = lax.broadcasted_iota(jnp.int32, (MB, MB), 0)
    return jnp.where(spot == inside, 1.0, 0.0)


def route_kernel(slot_ref, rows_ref, out_ref, token_ref):
    groups, modes, width = out_ref.shape
    per_tile = LANES // modes
    tiles = width // LANES
    owner = lax.broadcasted_iota(jnp.int32, (modes, LANES), 1) // modes

    def step(group, carry):
        for tile in range(tiles):
            block = jnp.zeros((modes, LANES), jnp.float32)
            for part in range(per_tile):
                slot = slot_ref[(group * tiles + tile) * per_tile + part]
                home = lax.shift_right_logical(slot, per_tile.bit_length() - 1)
                source = rows_ref[:, pl.ds(pl.multiple_of(home * LANES, LANES), LANES)]
                shift = ((part - slot) & (per_tile - 1)) * modes
                block = jnp.where(owner == part, pltpu.roll(source, shift, 1), block)
            out_ref[group, :, tile * LANES : (tile + 1) * LANES] = block
        return carry

    lax.fori_loop(0, groups, step, 0, unroll=2)
    token_ref[...] = jnp.zeros_like(token_ref)


def parities():
    return [lax.axis_index(axis) % 2 == 1 for axis in ("gy", "gx")]


def outgoing(field, refs):
    odd_column, odd_row = parities()
    west, east, south, north = (field[:, a:b] for a, b in sides(field.shape[1]))
    if len(refs) > 2:
        refs[0][...] = jnp.where(odd_row, north, south)
        refs[3][...] = jnp.where(odd_row, south, north)
        refs = refs[1:3]
    refs[0][...] = jnp.where(odd_column, east, west)
    refs[1][...] = jnp.where(odd_column, west, east)


def incoming(far, near, odd):
    return jnp.where(odd, near, far), jnp.where(odd, far, near)


def joined(field, others):
    odd_column, odd_row = parities()
    columns = others[1:3] if len(others) > 2 else others
    found = [*incoming(columns[0], columns[1], odd_column)]
    if len(others) > 2:
        found += incoming(others[0], others[3], odd_row)
    parts = [
        field[:, start:stop] + other for (start, stop), other in zip(sides(field.shape[1]), found)
    ]
    return jnp.concatenate(parts + [field[:, 2 * EW :]] * (len(others) == 2), axis=1)


def prepare_kernel(map_ref, basis_ref, loads_ref, token_ref, frame_ref, field_ref, *edge_refs):
    modes, cells = basis_ref.shape
    loads = loads_ref.shape[0]
    map_row = map_ref[...]
    both = jnp.concatenate([loads_ref[...], basis_ref[...]], axis=0)
    moved = jnp.concatenate(
        [
            dot(both[:, block * MB : (block + 1) * MB], one_hot(map_row, block), ((1,), (1,)))
            for block in range(cells // MB)
        ],
        axis=1,
    )
    high, low = split(moved[loads:])
    frame_ref[:modes, :] = high
    frame_ref[modes:, :] = low
    field_ref[...] = moved[:loads]
    outgoing(moved[:loads], edge_refs[1:3])
    odd_row = parities()[1]
    south, north = (moved[:, start:stop] for start, stop in sides(cells)[2:])
    edge_refs[0][...] = jnp.where(odd_row, north, south)
    edge_refs[3][...] = jnp.where(odd_row, south, north)


def reorder_kernel(map_ref, schur_ref, token_ref, high_ref, low_ref):
    cells = schur_ref.shape[0]
    map_row = map_ref[...]
    hots = [one_hot(map_row, block).astype(jnp.bfloat16) for block in range(cells // MB)]
    for i, left in enumerate(hots):
        span_i = slice(i * MB, (i + 1) * MB)
        for part, out_ref in zip(split(schur_ref[span_i, :]), (high_ref, low_ref)):
            rows = narrow_dot(left, part).astype(jnp.bfloat16)
            for j, right in enumerate(hots):
                span = slice(j * MB, (j + 1) * MB)
                out_ref[span_i, span] = narrow_dot(rows[:, span], right, ((1,), (1,))).astype(
                    jnp.bfloat16
                )


def stacked(value):
    return jnp.concatenate(split(value), axis=0)


def coefficients(field, frame):
    loads, modes = field.shape[0], frame.shape[0] // 2
    copies = [jnp.concatenate([part] * (LANES // loads), axis=0) for part in split(field)]
    both = narrow_dot(frame, jnp.concatenate(copies, axis=0), ((1,), (1,)))
    both = both[:, :LANES] + both[:, LANES:]
    return pack(both[:modes] + both[modes:], loads)


def flatten(coeffs, totals, out_ref):
    rows = [coeffs[quad : quad + 1, :] for quad in range(coeffs.shape[0])] + totals
    row = jnp.concatenate(rows, axis=1)
    out_ref[...] = jnp.broadcast_to(row[None], out_ref.shape)


def begin_kernel(own_ref, *refs):
    others = [ref[...] for ref in refs[:4]]
    frame_ref, residual_ref, out_ref, south_ref, north_ref = refs[4:]
    loads = own_ref.shape[0]
    south, north = incoming(others[0], others[3], parities()[1])
    south_ref[...] = stacked(south[loads:])
    north_ref[...] = stacked(north[loads:])
    field = joined(own_ref[...], [other[:loads] for other in others])
    residual_ref[...] = field
    coeffs = coefficients(field, frame_ref[...])
    flatten(coeffs, [jnp.zeros((1, LANES), jnp.float32)] * 2, out_ref)


def gather_kernel(more, own_ref, *refs):
    others = [ref[...] for ref in refs[:4]]
    residual_ref, refs = refs[4], refs[5:]
    out_ref = refs[-1]
    field = joined(own_ref[...], others)
    loads = field.shape[0]
    if more:
        frame_ref, field_ref = refs[:2]
        field_ref[...] = field
        coeffs = coefficients(field, frame_ref[...])
    else:
        coeffs = jnp.zeros((0, LANES), jnp.float32)
    totals = [
        row_of(jnp.sum(other * field, axis=1, keepdims=True), loads)
        for other in (residual_ref[...], field)
    ]
    flatten(coeffs, totals, out_ref)


def expanded(loads, gathered_ref, wide_ref):
    quads = wide_ref.shape[0] // (gathered_ref.shape[0] * ROWS)
    keep = sublane_mask(ROWS, loads)
    for column in range(gathered_ref.shape[0]):
        for quad in range(quads):
            row = gathered_ref[column, :, quad * LANES : (quad + 1) * LANES]
            start = (column * quads + quad) * ROWS
            wide_ref[start : start + ROWS, :] = jnp.where(keep, row, 0.0)
    wide = wide_ref[...]
    shift = LANES // 2
    while shift >= loads:
        wide = wide + pltpu.roll(wide, shift, 1)
        shift //= 2
    sums = jnp.sum(gathered_ref[:, :, quads * LANES :], axis=0)
    tail = jnp.concatenate(
        [sums[:, :LANES], sums[:, LANES:], jnp.zeros((2, LANES), jnp.float32)], axis=0
    )
    return jnp.concatenate(split(wide), axis=1), tail


def coarse_kernel(loads, first, *refs):
    if first:
        gathered_ref, matrix_ref, out_ref, high_ref, low_ref, wide_ref = refs
        high, low = split(matrix_ref[...])
        high_ref[...] = high
        low_ref[...] = low
    else:
        gathered_ref, high_ref, low_ref, out_ref, wide_ref = refs
        high, low = high_ref[...], low_ref[...]
    right, tail = expanded(loads, gathered_ref, wide_ref)
    groups = out_ref.shape[0]
    quads = high_ref.shape[0] // (groups * ROWS)
    product = narrow_dot(high, right) + narrow_dot(low, right)
    packed = pack(product[:, :LANES] + product[:, LANES:], loads)
    nothing = jnp.zeros((quads, LANES), jnp.float32)
    blocks = [packed[group * quads : (group + 1) * quads, :] for group in range(groups)]
    blocks = [nothing, *blocks, nothing]
    for group in range(groups):
        out_ref[group] = jnp.concatenate(
            [blocks[group + 1], blocks[group], blocks[group + 2], tail], axis=0
        )


def lift_kernel(iteration, *refs):
    refs = list(refs)
    reduced_ref, frame_ref, south_ref, north_ref, residual_ref = refs[:5]
    refs = refs[5:]
    residual = residual_ref[...]
    loads, cells = residual.shape
    quads = frame_ref.shape[0] // (2 * ROWS)
    sums = jnp.sum(reduced_ref[...], axis=0)
    lifted = sums
    if iteration:
        image_ref, search_ref, lifted_ref = refs[:3]
        refs = refs[3:]
        solution_ref = refs.pop(0) if iteration > 1 else None
        residual_out, solution_out = refs[:2]
        refs = refs[2:]
        stride_row = sums[3 * quads : 3 * quads + 1, :] / (
            sums[3 * quads + 1 : 3 * quads + 2, :] + epsilon
        )
        stride = column_of(stride_row, loads)
        residual = residual - stride * image_ref[...]
        residual_out[...] = residual
        step = stride * search_ref[...]
        solution_out[...] = step if solution_ref is None else solution_ref[...] + step
        lifted = lifted_ref[...] - stride_row * sums
    lifted_out, base_out, edges = refs[0], refs[1], refs[2:]
    lifted_out[...] = lifted
    keep = sublane_mask(ROWS, loads)
    a = lax.broadcasted_iota(jnp.int32, (loads, LANES), 0)
    b = lax.broadcasted_iota(jnp.int32, (loads, LANES), 1)
    fold = jnp.where(a == lax.rem(b, loads), 1.0, 0.0).astype(jnp.bfloat16)

    def spread(part, other_frame):
        rows = lifted[part * quads : (part + 1) * quads, :]
        wide = jnp.concatenate(
            [jnp.where(keep, rows[quad : quad + 1, :], 0.0) for quad in range(quads)], axis=0
        )
        left = jnp.concatenate(
            [
                jnp.concatenate([half, half], axis=1)
                for half in (
                    narrow_dot(fold, piece, ((1,), (1,))).astype(jnp.bfloat16)
                    for piece in split(wide)
                )
            ],
            axis=0,
        )
        both = narrow_dot(left, other_frame)
        return both[:loads] + both[loads:]

    own = spread(0, frame_ref[...])
    outgoing(own, edges)
    base = residual + own
    low, middle = sides(cells)[2]
    base_out[:, :low] = base[:, :low]
    base_out[:, low:middle] = base[:, low:middle] + spread(1, south_ref[...])
    base_out[:, middle:] = base[:, middle:] + spread(2, north_ref[...])


def schur_kernel(base_ref, first_ref, second_ref, high_ref, low_ref, search_ref, image_ref, *edges):
    search = joined(base_ref[...], [first_ref[...], second_ref[...]])
    search_ref[...] = search
    loads = search.shape[0]
    left = stacked(search)
    both = narrow_dot(left, high_ref[...]) + narrow_dot(left, low_ref[...])
    image = both[:loads] + both[loads:]
    image_ref[...] = image
    outgoing(image, edges)


def total_kernel(gathered_ref, out_ref):
    out_ref[...] = jnp.broadcast_to(jnp.sum(gathered_ref[...], axis=0)[None], out_ref.shape)


def finish_kernel(reduced_ref, solution_ref, search_ref, map_ref, out_ref):
    loads, cells = solution_ref.shape
    sums = jnp.sum(reduced_ref[...], axis=0)
    stride = column_of(sums[:, :LANES] / (sums[:, LANES:] + epsilon), loads)
    result = solution_ref[...] + stride * search_ref[...]
    map_row = map_ref[...]
    for block in range(cells // MB):
        span = slice(block * MB, (block + 1) * MB)
        out_ref[:, span] = dot(result[:, span], one_hot(map_row, block))


def exchange(edges):
    swaps = (("gx", 1), ("gy", 1), ("gy", 0), ("gx", 0))
    found = []
    chosen = swaps if len(edges) > 2 else swaps[1:3]
    for edge, (axis, start) in zip(edges, chosen):
        pairs = []
        for low in range(start, lax.axis_size(axis) - 1, 2):
            pairs += [(low, low + 1), (low + 1, low)]
        found.append(lax.ppermute(edge, axis, pairs))
    return found


def per_device(schur_blocks, basis, loads, coarse_inverse, iface_map, coarse_slot):
    f32, bf16 = jnp.float32, jnp.bfloat16
    columns = lax.axis_size("gy")
    groups = lax.axis_size("gx")
    count, cells = loads.shape[2:]
    modes = basis.shape[2]
    field = ((count, cells), f32)
    column_edges = [((count, EW), f32)] * 2
    row_edge = ((count, ES), f32)
    edges_of = [row_edge, *column_edges, row_edge]
    wide_edge = ((count + modes, ES), f32)
    packed = ((2 * ROWS, LANES), f32)
    along = ((columns, 1, (modes // ROWS + 2) * LANES), f32)
    along_last = ((columns, 1, 2 * LANES), f32)
    across = ((groups, 2 * ROWS, LANES), f32)

    routed, token = call(
        route_kernel,
        [((groups, modes, columns * modes), f32), ((ROWS, LANES), f32)],
        [coarse_slot, coarse_inverse],
        specs=[SMEM, VMEM],
    )
    matrix = lax.all_to_all(routed, "gx", 0, 0, tiled=True)
    matrix = matrix.reshape(groups * modes, columns * modes)

    frame, own, *edges = call(
        prepare_kernel,
        [((2 * modes, cells), bf16), field, wide_edge, *column_edges, wide_edge],
        [iface_map[0], basis[0, 0], loads[0, 0], token],
    )
    residual, payload, south, north = call(
        begin_kernel,
        [field, along] + [((2 * modes, ES), bf16)] * 2,
        [own, *exchange(edges), frame],
    )
    schur = call(
        reorder_kernel,
        [((cells, cells), bf16)] * 2,
        [iface_map[0], schur_blocks[0, 0], token],
        flops=1 << 28,
    )
    frames = [frame, south, north]
    split_shape = (matrix.shape, bf16)
    wide = [pltpu.VMEM((columns * modes, LANES), f32)]
    solution = image = search = lifted = None
    for iteration in range(ITERS):
        first = iteration == 0
        if first:
            payload, matrix, *schur = lax.optimization_barrier((payload, matrix, *schur))
        gathered = lax.all_to_all(payload, "gy", 0, 0, tiled=True)
        partial, *parts = call(
            functools.partial(coarse_kernel, count, first),
            [across] + [split_shape] * (2 * first),
            [gathered, matrix] if first else [gathered, *halves],
            flops=1 << 29,
            scratch=wide,
        )
        halves = parts if first else halves
        reduced = lax.all_to_all(partial, "gx", 0, 0, tiled=True)
        known = [image, search, lifted] if iteration else []
        found = call(
            functools.partial(lift_kernel, iteration),
            [field] * (2 if iteration else 0) + [packed, field, *column_edges],
            [reduced, *frames, residual, *known] + ([solution] if iteration > 1 else []),
        )
        if iteration:
            residual, solution, *found = found
        lifted, base, *edges = found
        search, local, *edges = call(
            schur_kernel,
            [field, field, *edges_of],
            [base, *exchange(edges), *schur],
            flops=1 << 27,
        )
        more = iteration < ITERS - 1
        found = call(
            functools.partial(gather_kernel, more),
            [field, along] if more else [along_last],
            [local, *exchange(edges), residual] + [frame] * more,
        )
        image, payload = found if more else (None, found[0])
    gathered = lax.all_to_all(payload, "gy", 0, 0, tiled=True)
    (partial,) = call(total_kernel, [((groups, 1, 2 * LANES), f32)], [gathered])
    reduced = lax.all_to_all(partial, "gx", 0, 0, tiled=True)
    (result,) = call(finish_kernel, [field], [reduced, solution, search, iface_map[0]])
    return result[None, None]


def solution(mesh):
    placed = (
        P("gx", "gy", None, None),
        P("gx", "gy", None, None),
        P("gx", "gy", None, None),
        P(("gx", "gy"), None),
        P("gx", "gy", None),
        P(),
    )
    return jax.shard_map(
        per_device, mesh=mesh, in_specs=placed, out_specs=P("gx", "gy", None, None), check_vma=False
    )
```
